32 devices in a mesh: rep: 4 (over x, core), space: 8 (over z, y).
Axes of the slice: x: 2, y: 2, z: 4, core: 2. Of those that a mesh axis runs over, the one named last changes fastest.
Arguments:
- phase_space: float32 [4, 6, 4, 16384], P('rep', None, None, 'space'), may hold values from -6 to 6
- charges: float32 [4, 4, 16384], P('rep', None, 'space'), may hold values from -4 to 4
- lj_depth: float32 [4, 4, 16384], P('rep', None, 'space'), may hold values from 0.5 to 2
- cluster_fill: int32 [4, 16384], P('rep', 'space'), may hold values from 1 to 4
- neighbours: int32 [4, 16, 16384], P('rep', None, 'space'), may hold values from 0 to 3071
- ghost_send: int32 [4, 8192], P('rep', 'space'), may hold values from 0 to 2047
- partner: int32 [4], replicated, may hold values from 0 to 3, as said below
- scale_order: int32 [4], replicated, may hold values from 0 to 3, as said below
- coupling: float32 [4], replicated, may hold values from 0.25 to 1
Outputs:
- advanced: float32 [4, 6, 4, 16384], P('rep', None, None, 'space')
The draws below stay inside these ranges and needn't reach their ends.
Inputs may be any that keep to these rules, and one draw needn't show every extreme that they name: partner[l] is l - 1, l or l + 1, and partner[partner[l]] = l; for one p of 0 or 1, the same for the whole matching, every swapped pair is (2k + p, 2k + p + 1). `scale_order`: each level once.
All inputs are finite; a program needn't handle non-finite values.
Results may differ from the reference program's by a relative error of at most 0.0003.
Values sent between devices are 32-bit elements; how exact they have to be, the bound alone decides.
A program may use at most 128 MiB of HBM per device.

```python
import math
import jax
import jax.numpy as jnp
from jax import lax

CS = 4
NB = 16
STEPS = 2
NCL = 2048
LEVELS = 4
GHOST = 512
NCLT = 16384
N_SPACE = 8


def draw_partner(key, part):
    phase_bit = jax.random.randint(jax.random.fold_in(key, 11), (), 0, 2)
    accepted = jax.random.randint(jax.random.fold_in(key, 12), (LEVELS,), 0, 2)
    levels = jnp.arange(LEVELS, dtype=jnp.int32)
    pair_low = levels - (levels - phase_bit) % 2
    usable = (pair_low >= 0) & (pair_low + 1 < LEVELS)
    taken = (accepted[jnp.clip(pair_low, 0, LEVELS - 1)] == 1) & usable
    moved = jnp.where(levels == pair_low, levels + 1, levels - 1)
    return jnp.where(taken, moved, levels).astype(jnp.int32)


def draw_scale_order(key, part):
    order = jax.random.permutation(jax.random.fold_in(key, 21), LEVELS).astype(jnp.int32)
    target = jax.random.randint(jax.random.fold_in(key, 22), (), 2, LEVELS).astype(jnp.int32)
    levels = jnp.arange(LEVELS, dtype=jnp.int32)
    holder = jnp.sum(jnp.where(order == target, levels, 0)).astype(jnp.int32)
    first = order[0]
    result = jnp.where(levels == 0, target, jnp.where(levels == holder, first, order))
    return result.astype(jnp.int32)


def touch_ends(values, own_key, least, largest):
    longest = values.shape.index(max(values.shape))
    spots = []
    for shift in (0, 1):
        where = [jax.random.randint(jax.random.fold_in(own_key, axis), (), 0, length) for axis, length in enumerate(values.shape)]
        where[longest] = (where[longest] + shift) % values.shape[longest]
        spots.append(tuple(where))
    return values.at[spots[0]].set(least).at[spots[1]].set(largest)


def level_of(key, extent, shards, low, top_value):
    factor_of, own = 1.0, jax.random.fold_in(key, 6)
    for axis_at, blocks in shards:
        draws = jnp.exp(jax.random.uniform(jax.random.fold_in(own, axis_at), (blocks,), jnp.float32, low / len(shards), top_value / len(shards)))
        factor_of = factor_of * jnp.repeat(draws, extent[axis_at] // blocks).reshape([-1 if axis == axis_at else 1 for axis in range(len(extent))])
    return factor_of


def scatter_about(rng, shape, scale, bound, pieces=(), kind=jnp.bfloat16):
    gain = level_of(rng, shape, pieces, -0.22, 0.18) if pieces else 1.0
    array = jax.random.normal(rng, shape, jnp.float32) * scale * gain
    return jnp.minimum(jnp.maximum(array, -bound), bound).astype(kind)


def setup_inputs(seed: int = 0) -> dict:
    streams_of = jax.random.split(jax.random.key(seed), 10)
    return {
        "phase_space": scatter_about(streams_of[0], (LEVELS, 6, CS, NCLT), 1.0, 6.0, ((0, 4), (3, 8)), jnp.float32),
        "charges": scatter_about(streams_of[1], (LEVELS, CS, NCLT), 1.0, 4.0, ((0, 4), (2, 8)), jnp.float32),
        "lj_depth": jnp.clip(jnp.exp(math.log(2.0) - 1.3862944 * jax.random.uniform(streams_of[2], (LEVELS, CS, NCLT), jnp.float32) ** level_of(streams_of[2], (LEVELS, CS, NCLT), ((0, 4), (2, 8)), -0.2, 0.2)), 0.5, 2.0),
        "cluster_fill": touch_ends(jax.random.randint(streams_of[3], (LEVELS, NCLT), 1, 5), jax.random.fold_in(streams_of[3], 1), 1, 4).astype(jnp.int32),
        "neighbours": touch_ends(jax.random.randint(streams_of[4], (LEVELS, NB, NCLT), 0, NCL + 2 * GHOST), jax.random.fold_in(streams_of[4], 1), 0, (NCL + 2 * GHOST) - 1).astype(jnp.int32),
        "ghost_send": touch_ends(jax.random.randint(streams_of[5], (LEVELS, 2 * GHOST * N_SPACE), 0, NCL), jax.random.fold_in(streams_of[5], 1), 0, NCL - 1).astype(jnp.int32),
        "partner": draw_partner(jax.random.fold_in(streams_of[9], 71), 0),
        "scale_order": draw_scale_order(jax.random.fold_in(streams_of[9], 71), 0),
        "coupling": jnp.clip(jnp.exp(jax.random.uniform(streams_of[8], (LEVELS,), jnp.float32, math.log(0.25), math.log(1.0))), 0.25, 1.0),
    }


time_step = 0.2
softening = 0.5

def cluster_forces(positions, params, pool_pos, pool_par, near_list, strength):
    total = positions.shape[2]
    block_size = min(512, total)
    block_count = total // block_size

    def block_forces(block_id):
        first_row = (block_id * block_size).astype(jnp.int32)
        own_pos = lax.dynamic_slice_in_dim(positions, first_row, block_size, 2)
        own_par = lax.dynamic_slice_in_dim(params, first_row, block_size, 2)
        slot_ids = lax.dynamic_slice_in_dim(near_list, first_row, block_size, 1)
        other_pos = pool_pos[:, :, slot_ids]
        other_par = pool_par[:, :, slot_ids]
        offset = own_pos[:, :, None, None, :] - other_pos[:, None]
        inverse = 1.0 / (lax.optimization_barrier(jnp.sum(offset * offset, axis=0)) + softening)
        charge_pair = own_par[0][:, None, None, :] * other_par[0][None]
        depth_pair = own_par[1][:, None, None, :] * other_par[1][None]
        weight = strength * charge_pair * inverse * jnp.sqrt(inverse) + depth_pair * (inverse ** 3 - inverse ** 2)
        return lax.optimization_barrier(jnp.sum(weight[None] * offset, axis=(2, 3)))
    stacked = lax.map(block_forces, jnp.arange(block_count, dtype=jnp.int32))
    return jnp.moveaxis(stacked, 0, 2).reshape(3, positions.shape[1], total)

def reference(phase_space, charges, lj_depth, cluster_fill, neighbours, ghost_send, partner, scale_order, coupling):
    swapped = phase_space[partner]
    couplings = coupling[scale_order]
    send_lists = ghost_send.reshape(LEVELS, N_SPACE, 2 * GHOST)

    def run_level(level_data):
        phase_now, charge_row, depth_row, fill_row, near_level, sender_level, strength = level_data
        atom_slot = jnp.arange(CS, dtype=jnp.int32)[:, None]
        present = (atom_slot < fill_row[None, :]).astype(jnp.float32)
        params = jnp.stack([charge_row * present, depth_row * present]).reshape(2, CS, N_SPACE, NCL)
        phase_now = phase_now.reshape(6, CS, N_SPACE, NCL)
        positions = phase_now[:3]
        velocity = phase_now[3:]
        near_level = near_level.reshape(NB, N_SPACE, NCL)
        for step_index in range(STEPS):
            packet = jnp.concatenate([positions, params], 0)

            def device_forces(device):
                lower = (device - 1) % N_SPACE
                upper = (device + 1) % N_SPACE
                from_lower = jnp.take(packet[:, :, lower], sender_level[lower][GHOST:], axis=2)
                from_upper = jnp.take(packet[:, :, upper], sender_level[upper][:GHOST], axis=2)
                pool = jnp.concatenate([packet[:, :, device], from_lower, from_upper], 2)
                return cluster_forces(positions[:, :, device], params[:, :, device], pool[:3], pool[3:], near_level[:, device], strength)
            forces = lax.map(device_forces, jnp.arange(N_SPACE, dtype=jnp.int32))
            forces = jnp.moveaxis(forces, 0, 2)
            velocity = velocity + time_step * forces
            positions = positions + time_step * velocity
        return jnp.concatenate([positions, velocity], 0).reshape(6, CS, N_SPACE * NCL)
    return lax.map(run_level, (swapped, charges, lj_depth, cluster_fill, neighbours, send_lists, couplings))
```

```python
import functools

import jax
import jax.numpy as jnp
from jax import lax
from jax.experimental import pallas as pl
from jax.experimental.pallas import tpu as pltpu
from jax.sharding import PartitionSpec as P

STEPS = 2
LANES = 128

time_step = 0.2
softening = 0.5

VMEM = pl.BlockSpec(memory_space=pltpu.VMEM)
SMEM = pl.BlockSpec(memory_space=pltpu.SMEM)
f32 = jnp.float32


def upper_half():
    return lax.broadcasted_iota(jnp.int32, (8, LANES), 0) >= 4


def row(values):
    return jnp.broadcast_to(values, (8, LANES))


def fill_table(tab, c, first, block):
    for k in range(block.shape[1] // LANES):
        tile = block[:, k * LANES : (k + 1) * LANES]
        tab[c, first + k] = jnp.concatenate([tile, tile], 0)


def lookup(tab, comps, tiles, index):
    low = index & (LANES - 1)
    high = index >> 7
    found = [None] * len(comps)
    for k in range(tiles):
        mask = high == k
        for n, c in enumerate(comps):
            got = jnp.take_along_axis(tab[c, k], low, axis=1)
            found[n] = got if k == 0 else jnp.where(mask, got, found[n])
    return found


def send_ghosts(tab, comps, tiles, gs, out_first, out_last):
    width = out_first.shape[2]
    up = upper_half()
    for g in range(width // LANES):
        index = jnp.where(
            up,
            row(gs[:, width + g * LANES : width + (g + 1) * LANES]),
            row(gs[:, g * LANES : (g + 1) * LANES]),
        )
        for c, got in zip(range(comps), lookup(tab, range(comps), tiles, index)):
            out_first[c, :, g * LANES : (g + 1) * LANES] = got[:4]
            out_last[c, :, g * LANES : (g + 1) * LANES] = got[4:]


def params_kernel(charges, lj, fill, gs, par, out_first, out_last, tab):
    total = charges.shape[1]
    slot = lax.broadcasted_iota(jnp.int32, (4, total), 0)
    present = (slot < fill[...]).astype(f32)
    par[0] = charges[...] * present
    par[1] = lj[...] * present
    for c in range(2):
        fill_table(tab, c, 0, par[c])
    send_ghosts(tab, 2, total // LANES, gs, out_first, out_last)


def swap_kernel(sel, mine, low, high, gs, pos, out_first, out_last, tab):
    total = mine.shape[2]
    which = sel[0]
    for c in range(3):
        block = jnp.where(which == 0, mine[c], jnp.where(which < 0, low[c], high[c]))
        pos[c] = block
        fill_table(tab, c, 0, block)
    send_ghosts(tab, 3, total // LANES, gs, out_first, out_last)


def pair_index(near, pair, base):
    return jnp.where(
        upper_half(),
        row(near[2 * pair + 1 : 2 * pair + 2, pl.ds(base, LANES)]),
        row(near[2 * pair : 2 * pair + 1, pl.ds(base, LANES)]),
    )


def gather_kernel(par, from_low, from_high, near, out, tab):
    total, width = par.shape[2], from_low.shape[2]
    own, ghost = total // LANES, width // LANES
    for c in range(2):
        fill_table(tab, c, 0, par[c])
        fill_table(tab, c, own, from_low[c])
        fill_table(tab, c, own + ghost, from_high[c])
    tiles = own + 2 * ghost

    def body(group, carry):
        base = pl.multiple_of(group * LANES, LANES)
        for pair in range(near.shape[0] // 2):
            got = lookup(tab, (0, 1), tiles, pair_index(near, pair, base))
            out[group, pair, 0] = got[0]
            out[group, pair, 1] = got[1]
        return carry

    lax.fori_loop(0, own, body, 0)


def step_body(strength, pos, from_low, from_high, par, gathered, near, velocity, new_pos, new_vel, tab):
    total, width = pos.shape[2], from_low.shape[2]
    own, ghost = total // LANES, width // LANES
    for c in range(3):
        fill_table(tab, c, 0, pos[c])
        fill_table(tab, c, own, from_low[c])
        fill_table(tab, c, own + ghost, from_high[c])
    tiles = own + 2 * ghost
    scale = strength[0]

    def body(group, carry):
        base = pl.multiple_of(group * LANES, LANES)
        lanes = pl.ds(base, LANES)
        force = [[None] * 4 for _ in range(3)]
        for pair in range(near.shape[0] // 2):
            there = lookup(tab, (0, 1, 2), tiles, pair_index(near, pair, base))
            charge = gathered[group, pair, 0] * scale
            depth = gathered[group, pair, 1]
            for i in range(4):
                offset = [row(pos[c, i : i + 1, lanes]) - there[c] for c in range(3)]
                square = offset[0] * offset[0] + offset[1] * offset[1] + offset[2] * offset[2]
                root = lax.rsqrt(square + softening)
                w = root * root
                qq = row(par[0, i : i + 1, lanes]) * charge
                ee = row(par[1, i : i + 1, lanes]) * depth
                weight = w * (qq * root + ee * (w * w - w))
                for c in range(3):
                    term = weight * offset[c]
                    force[c][i] = term if pair == 0 else force[c][i] + term
        for c in range(3):
            rows = [jnp.sum(force[c][i], axis=0, keepdims=True) for i in range(4)]
            v = velocity(c, lanes) + time_step * jnp.concatenate(rows, 0)
            new_vel(c, lanes, v)
            new_pos(c, lanes, pos[c, :, lanes] + time_step * v)
        return carry

    lax.fori_loop(0, own, body, 0)


def first_step_kernel(
    sel, strength, pos, from_low, from_high, par, gathered, near, mine, low, high, gs,
    pos_out, vel_out, out_first, out_last, tab,
):
    which = sel[0]

    def velocity(c, lanes):
        return jnp.where(
            which == 0, mine[c, :, lanes],
            jnp.where(which < 0, low[c, :, lanes], high[c, :, lanes]),
        )

    def new_vel(c, lanes, v):
        vel_out[c, :, lanes] = v

    def new_pos(c, lanes, v):
        pos_out[c, :, lanes] = v

    step_body(strength, pos, from_low, from_high, par, gathered, near, velocity, new_pos, new_vel, tab)
    total = pos.shape[2]
    for c in range(3):
        fill_table(tab, c, 0, pos_out[c])
    send_ghosts(tab, 3, total // LANES, gs, out_first, out_last)


def last_step_kernel(
    strength, pos, from_low, from_high, par, gathered, near, vel, out, tab
):
    def velocity(c, lanes):
        return vel[c, :, lanes]

    def new_vel(c, lanes, v):
        out[3 + c, :, lanes] = v

    def new_pos(c, lanes, v):
        out[c, :, lanes] = v

    step_body(strength, pos, from_low, from_high, par, gathered, near, velocity, new_pos, new_vel, tab)


def call(kernel, outs, args, smem, comps, tiles, flops=0):
    return pl.pallas_call(
        kernel,
        out_shape=[jax.ShapeDtypeStruct(s, f32) for s in outs],
        in_specs=[SMEM] * smem + [VMEM] * (len(args) - smem),
        out_specs=[VMEM] * len(outs),
        scratch_shapes=[pltpu.VMEM((comps, tiles, 8, LANES), f32)],
        cost_estimate=pl.CostEstimate(flops=flops, bytes_accessed=1 << 20, transcendentals=0),
    )(*args)


def on_device(
    phase_space, charges, lj_depth, cluster_fill, neighbours, ghost_send, partner, scale_order, coupling
):
    phase = phase_space[0]
    slots, total = phase.shape[1:]
    width = ghost_send.shape[1] // 2
    near = neighbours[0]
    level, levels = lax.axis_index("rep"), lax.axis_size("rep")
    spaces = lax.axis_size("space")
    up = [(i, i + 1) for i in range(levels - 1)]
    down = [(i + 1, i) for i in range(levels - 1)]
    ring_up = [(i, (i + 1) % spaces) for i in range(spaces)]
    ring_down = [(b, a) for a, b in ring_up]

    def to_neighbours(first, last):
        return lax.ppermute(last, "space", ring_up), lax.ppermute(first, "space", ring_down)

    mine_pos, mine_vel = phase[:3], phase[3:]
    pos_low, pos_high = lax.ppermute(mine_pos, "rep", up), lax.ppermute(mine_pos, "rep", down)
    vel_low, vel_high = lax.ppermute(mine_vel, "rep", up), lax.ppermute(mine_vel, "rep", down)
    sel = (partner[level] - level).astype(jnp.int32).reshape(1)
    strength = coupling[scale_order[level]].reshape(1)

    own = total // LANES
    tiles = own + 2 * (width // LANES)
    ghosts = lambda comps: [(comps, slots, width)] * 2
    pairs = near.shape[0] // 2

    par, first, last = call(
        params_kernel, [(2, slots, total)] + ghosts(2),
        (charges[0], lj_depth[0], cluster_fill, ghost_send), 0, 2, own,
    )
    par_low, par_high = to_neighbours(first, last)
    pos, first, last = call(
        swap_kernel, [(3, slots, total)] + ghosts(3),
        (sel, mine_pos, pos_low, pos_high, ghost_send), 1, 3, own,
    )
    ghost_low, ghost_high = to_neighbours(first, last)
    (gathered,) = call(
        gather_kernel, [(own, pairs, 2, 8, LANES)], (par, par_low, par_high, near), 0, 2, tiles, 1 << 24
    )
    pos, vel, first, last = call(
        first_step_kernel, [(3, slots, total)] * 2 + ghosts(3),
        (sel, strength, pos, ghost_low, ghost_high, par, gathered, near, mine_vel, vel_low, vel_high, ghost_send),
        2, 3, tiles, 1 << 25,
    )
    ghost_low, ghost_high = to_neighbours(first, last)
    (out,) = call(
        last_step_kernel, [(6, slots, total)],
        (strength, pos, ghost_low, ghost_high, par, gathered, near, vel), 1, 3, tiles, 1 << 25,
    )
    return out[None]


def solution(mesh):
    return jax.shard_map(
        on_device,
        mesh=mesh,
        in_specs=(
            P("rep", None, None, "space"),
            P("rep", None, "space"),
            P("rep", None, "space"),
            P("rep", "space"),
            P("rep", None, "space"),
            P("rep", "space"),
            P(),
            P(),
            P(),
        ),
        out_specs=P("rep", None, None, "space"),
        check_vma=False,
    )
```

```python
import jax
import jax.numpy as jnp
from jax import lax
from jax.experimental import pallas as pl
from jax.experimental.pallas import tpu as pltpu
from jax.sharding import PartitionSpec as P

STEPS = 2
LANES = 128

time_step = 0.2
softening = 0.5

VMEM = pl.BlockSpec(memory_space=pltpu.VMEM)
SMEM = pl.BlockSpec(memory_space=pltpu.SMEM)
MESH = pl.DeviceIdType.MESH
f32 = jnp.float32
i32 = jnp.int32

POS = float((1 << 20) - 2)
LOW = (1 << 11) - 1
Q_STEPS = 8191.0
E_STEPS = 32767.0


def upper_half():
    return lax.broadcasted_iota(i32, (8, LANES), 0) >= 4


def row(values):
    return jnp.broadcast_to(values, (8, LANES))


def twice(tile):
    return jnp.concatenate([tile, tile], 0)


def lookup(tabs, first, count, low, high):
    bits = max(count - 1, 0).bit_length()
    masks = [(high & (1 << b)) != 0 for b in range(bits)]

    def find(tab, bit, start):
        if bit < 0:
            return jnp.take_along_axis(tab[first + start], low, axis=1)
        lower = find(tab, bit - 1, start)
        if start + (1 << bit) >= count:
            return lower
        return jnp.where(masks[bit], find(tab, bit - 1, start + (1 << bit)), lower)

    return [find(tab, bits - 1, 0) for tab in tabs]


def find_in_pool(tabs, own, tiles, index):
    low, high = index & (LANES - 1), index >> 7
    here = lookup(tabs, 0, own, low, high)
    there = lookup(tabs, own, tiles - own, low, high - own)
    return [jnp.where(high < own, a, b) for a, b in zip(here, there)]


def pair_index(near, pair, base):
    return jnp.where(
        upper_half(),
        row(near[2 * pair + 1 : 2 * pair + 2, pl.ds(base, LANES)]),
        row(near[2 * pair : 2 * pair + 1, pl.ds(base, LANES)]),
    )


def fill_exact(tab, block):
    for k in range(block.shape[1] // LANES):
        tab[k] = twice(block[:, k * LANES : (k + 1) * LANES])


def gather_ghosts(tab, comps, own, gs, out_first, out_last):
    width = out_first.shape[2]
    up = upper_half()
    for g in range(width // LANES):
        index = jnp.where(
            up,
            row(gs[:, width + g * LANES : width + (g + 1) * LANES]),
            row(gs[:, g * LANES : (g + 1) * LANES]),
        )
        found = lookup([tab.at[c] for c in range(comps)], 0, own, index & (LANES - 1), index >> 7)
        for c in range(comps):
            out_first[c, :, g * LANES : (g + 1) * LANES] = found[c][:4]
            out_last[c, :, g * LANES : (g + 1) * LANES] = found[c][4:]


def pack_params(tab, first, par):
    for k in range(par.shape[2] // LANES):
        cut = slice(k * LANES, (k + 1) * LANES)
        q = (par[0, :, cut] * Q_STEPS + 32768.5).astype(i32) - 32768
        e = (par[1, :, cut] * E_STEPS + 0.5).astype(i32)
        tab[first + k] = twice((q << 16) | e)


def largest(blocks):
    top = None
    for block in blocks:
        for c in range(3):
            here = jnp.max(jnp.abs(block[c]), axis=0, keepdims=True)
            here = jnp.max(here, axis=1, keepdims=True)
            top = here if top is None else jnp.maximum(top, here)
    return jnp.maximum(top, 1e-30)


def pack_positions(tabs, first, pos, top):
    factor = POS / top
    for k in range(pos.shape[2] // LANES):
        cut = slice(k * LANES, (k + 1) * LANES)
        x = (pos[0, :, cut] * factor + (1048576.5)).astype(i32) - 1048576
        y = (pos[1, :, cut] * factor + (1048576.5)).astype(i32) - 1048576
        z = (pos[2, :, cut] * factor * 2.0 + (2097152.5)).astype(i32)
        tabs[0][first + k] = twice((x << 11) | (z >> 11))
        tabs[1][first + k] = twice((y << 11) | (z & LOW))


def unpack_positions(words, unit):
    x = (words[0] >> 11).astype(f32) * unit
    y = (words[1] >> 11).astype(f32) * unit
    z = (((words[0] & LOW) << 11) | (words[1] & LOW)).astype(f32)
    return x, y, (z - 2097152.0) * (0.5 * unit)


def forces(pos, par, base, found, charges, depths):
    lanes = pl.ds(base, LANES)
    force = [[None] * 4 for _ in range(3)]
    for pair in range(len(charges)):
        there = found(pair)
        charge, depth = charges[pair], depths[pair]
        for i in range(4):
            offset = [row(pos[c, i : i + 1, lanes]) - there[c] for c in range(3)]
            square = offset[0] * offset[0] + offset[1] * offset[1] + offset[2] * offset[2]
            root = lax.rsqrt(square + softening)
            w = root * root
            qq = row(par[0, i : i + 1, lanes]) * charge
            ee = row(par[1, i : i + 1, lanes]) * depth
            weight = w * (qq * root + ee * (w * w - w))
            for c in range(3):
                term = weight * offset[c]
                force[c][i] = term if pair == 0 else force[c][i] + term
    return [
        jnp.concatenate([jnp.sum(force[c][i], axis=0, keepdims=True) for i in range(4)], 0)
        for c in range(3)
    ]


def kernel(
    partner, scale_order, coupling, phase, charges, lj, fill, near, gs, out,
    from_low, from_high, par, par_first, par_last, par_low, par_high,
    pos_first, pos_last, pos_low, pos_high, pos, pos_next, vel,
    exact, packed_par, packed_pos, gathered, part, send_sem, recv_sem,
):
    total, width = phase.shape[2], gs.shape[1] // 2
    own, ghost = total // LANES, width // LANES
    tiles = own + 2 * ghost
    pairs = near.shape[0] // 2
    level, levels = lax.axis_index("rep"), lax.axis_size("rep")
    place, places = lax.axis_index("space"), lax.axis_size("space")
    has_low, has_high = level > 0, level < levels - 1
    above, below = lax.rem(place + 1, places), lax.rem(place + places - 1, places)

    barrier = pltpu.get_barrier_semaphore()

    def greet(device):
        pl.semaphore_signal(barrier, inc=1, device_id=device, device_id_type=MESH)

    greet({"space": above})
    greet({"space": below})

    @pl.when(has_low)
    def _():
        greet({"rep": level - 1})

    @pl.when(has_high)
    def _():
        greet({"rep": level + 1})

    pl.semaphore_wait(barrier, 2 + jnp.where(has_low, 1, 0) + jnp.where(has_high, 1, 0))

    def remote(src, dst, number, device):
        return pltpu.make_async_remote_copy(
            src_ref=src, dst_ref=dst, send_sem=send_sem.at[number], recv_sem=recv_sem.at[number],
            device_id=device, device_id_type=MESH,
        )

    halves = (pl.ds(0, 3), pl.ds(3, 3))
    rising = [remote(phase.at[h], from_low.at[h], n, {"rep": level + 1}) for n, h in enumerate(halves)]
    falling = [remote(phase.at[h], from_high.at[h], 2 + n, {"rep": level - 1}) for n, h in enumerate(halves)]

    for n in range(2):

        @pl.when(has_high)
        def _():
            rising[n].start()

        @pl.when(has_low)
        def _():
            falling[n].start()

    def swap_arrived(n):
        @pl.when(has_low)
        def _():
            rising[n].wait_recv()

        @pl.when(has_high)
        def _():
            falling[n].wait_recv()

    def ring(first, last, low, high, number):
        return [remote(last, low, number, {"space": above}), remote(first, high, number + 1, {"space": below})]

    slot = lax.broadcasted_iota(i32, (4, total), 0)
    present = (slot < fill[...]).astype(f32)
    par[0] = charges[...] * present
    par[1] = lj[...] * present
    for c in range(2):
        fill_exact(exact.at[c], par[c])
    gather_ghosts(exact, 2, own, gs, par_first, par_last)
    par_ring = ring(par_first, par_last, par_low, par_high, 4)
    for copy in par_ring:
        copy.start()
    pack_params(packed_par, 0, par)

    moved = partner[level] - level

    def swapped(c, lanes):
        return jnp.where(
            moved == 0, phase[c, :, lanes],
            jnp.where(moved < 0, from_low[c, :, lanes], from_high[c, :, lanes]),
        )

    swap_arrived(0)
    for c in range(3):
        block = swapped(c, pl.ds(0, total))
        pos[c] = block
        fill_exact(exact.at[c], block)
    gather_ghosts(exact, 3, own, gs, pos_first.at[0], pos_last.at[0])
    pos_rings = [
        ring(pos_first.at[n], pos_last.at[n], pos_low.at[n], pos_high.at[n], 6 + 2 * n) for n in range(2)
    ]
    for copy in pos_rings[0]:
        copy.start()
    tabs = [packed_pos.at[0], packed_pos.at[1]]
    top_own = largest([pos])
    pack_positions(tabs, 0, pos, top_own)
    unit_own = top_own * (1.0 / POS)

    for copy in par_ring:
        copy.wait_recv()
    pack_params(packed_par, own, par_low)
    pack_params(packed_par, own + ghost, par_high)
    strength = coupling[scale_order[level]] * (1.0 / Q_STEPS)

    def gather_params(group, carry):
        base = pl.multiple_of(group * LANES, LANES)
        for pair in range(pairs):
            (word,) = find_in_pool([packed_par], own, tiles, pair_index(near, pair, base))
            gathered[group, pair, 0] = (word >> 16).astype(f32) * strength
            gathered[group, pair, 1] = (word & 65535).astype(f32) * (1.0 / E_STEPS)
        return carry

    lax.fori_loop(0, own, gather_params, 0)

    def ghosts_arrived(n):
        for copy in pos_rings[n]:
            copy.wait_recv()
        low, high = pos_low.at[n], pos_high.at[n]
        top = largest([low, high])
        pack_positions(tabs, own, low, top)
        pack_positions(tabs, own + ghost, high, top)
        return top * (1.0 / POS)

    def params_of(group):
        return (
            [gathered[group, pair, 0] for pair in range(pairs)],
            [gathered[group, pair, 1] for pair in range(pairs)],
        )

    swap_arrived(1)
    unit_ghost = ghosts_arrived(0)

    def first_step(group, carry):
        base = pl.multiple_of(group * LANES, LANES)
        lanes = pl.ds(base, LANES)

        def found(pair):
            index = pair_index(near, pair, base)
            words = find_in_pool(tabs, own, tiles, index)
            return unpack_positions(words, jnp.where(index < total, unit_own, unit_ghost))

        force = forces(pos, par, base, found, *params_of(group))
        for c in range(3):
            v = swapped(3 + c, lanes) + time_step * force[c]
            vel[c, :, lanes] = v
            pos_next[c, :, lanes] = pos[c, :, lanes] + time_step * v
        return carry

    lax.fori_loop(0, own, first_step, 0)

    for c in range(3):
        fill_exact(exact.at[c], pos_next[c])
    gather_ghosts(exact, 3, own, gs, pos_first.at[1], pos_last.at[1])
    for copy in pos_rings[1]:
        copy.start()
    top_own = largest([pos_next])
    pack_positions(tabs, 0, pos_next, top_own)
    unit_own_next = top_own * (1.0 / POS)

    def own_part(group, carry):
        base = pl.multiple_of(group * LANES, LANES)
        for pair in range(pairs):
            index = pair_index(near, pair, base)
            words = lookup(tabs, 0, own, index & (LANES - 1), index >> 7)
            part[group, pair, 0] = words[0]
            part[group, pair, 1] = words[1]
        return carry

    lax.fori_loop(0, own, own_part, 0)
    unit_ghost_next = ghosts_arrived(1)

    def second_step(group, carry):
        base = pl.multiple_of(group * LANES, LANES)
        lanes = pl.ds(base, LANES)

        def found(pair):
            index = pair_index(near, pair, base)
            words = lookup(tabs, own, tiles - own, index & (LANES - 1), (index >> 7) - own)
            here = index < total
            words = [jnp.where(here, part[group, pair, n], words[n]) for n in range(2)]
            return unpack_positions(words, jnp.where(here, unit_own_next, unit_ghost_next))

        force = forces(pos_next, par, base, found, *params_of(group))
        for c in range(3):
            v = vel[c, :, lanes] + time_step * force[c]
            out[3 + c, :, lanes] = v
            out[c, :, lanes] = pos_next[c, :, lanes] + time_step * v
        return carry

    lax.fori_loop(0, own, second_step, 0)

    for copy in par_ring + pos_rings[0] + pos_rings[1]:
        copy.wait_send()
    for n in range(2):

        @pl.when(has_high)
        def _():
            rising[n].wait_send()

        @pl.when(has_low)
        def _():
            falling[n].wait_send()


def on_device(
    phase_space, charges, lj_depth, cluster_fill, neighbours, ghost_send, partner, scale_order, coupling
):
    phase = phase_space[0]
    rows, slots, total = phase.shape
    width = ghost_send.shape[1] // 2
    own = total // LANES
    tiles = own + 2 * (width // LANES)
    pairs = neighbours.shape[1] // 2
    out = pl.pallas_call(
        kernel,
        out_shape=jax.ShapeDtypeStruct(phase.shape, f32),
        in_specs=[SMEM] * 3 + [VMEM] * 6,
        out_specs=VMEM,
        scratch_shapes=[
            pltpu.VMEM((rows, slots, total), f32),
            pltpu.VMEM((rows, slots, total), f32),
            pltpu.VMEM((2, slots, total), f32),
        ]
        + [pltpu.VMEM((2, slots, width), f32)] * 4
        + [pltpu.VMEM((2, 3, slots, width), f32)] * 4
        + [pltpu.VMEM((3, slots, total), f32)] * 3
        + [
            pltpu.VMEM((3, own, 8, LANES), f32),
            pltpu.VMEM((tiles, 8, LANES), i32),
            pltpu.VMEM((2, tiles, 8, LANES), i32),
            pltpu.VMEM((own, pairs, 2, 8, LANES), f32),
            pltpu.VMEM((own, pairs, 2, 8, LANES), i32),
            pltpu.SemaphoreType.DMA((10,)),
            pltpu.SemaphoreType.DMA((10,)),
        ],
        compiler_params=pltpu.CompilerParams(collective_id=0, has_side_effects=True),
    )(partner, scale_order, coupling, phase, charges[0], lj_depth[0], cluster_fill, neighbours[0], ghost_send)
    return out[None]


def solution(mesh):
    return jax.shard_map(
        on_device,
        mesh=mesh,
        in_specs=(
            P("rep", None, None, "space"),
            P("rep", None, "space"),
            P("rep", None, "space"),
            P("rep", "space"),
            P("rep", None, "space"),
            P("rep", "space"),
            P(),
            P(),
            P(),
        ),
        out_specs=P("rep", None, None, "space"),
        check_vma=False,
    )
```

```python
import jax
import jax.numpy as jnp
from jax import lax
from jax.experimental import pallas as pl
from jax.experimental.pallas import tpu as pltpu
from jax.sharding import PartitionSpec as P

STEPS = 2
LANES = 128

time_step = 0.2
softening = 0.5

VMEM = pl.BlockSpec(memory_space=pltpu.VMEM)
SMEM = pl.BlockSpec(memory_space=pltpu.SMEM)
MESH = pl.DeviceIdType.MESH
f32 = jnp.float32
i32 = jnp.int32

POS = float((1 << 20) - 2)
LOW = (1 << 11) - 1
Q_STEPS = 8191.0
E_STEPS = 32767.0


def upper_half():
    return lax.broadcasted_iota(i32, (8, LANES), 0) >= 4


def row(values):
    return jnp.broadcast_to(values, (8, LANES))


def twice(tile):
    return jnp.concatenate([tile, tile], 0)


def lookup(tabs, first, count, low, high):
    bits = max(count - 1, 0).bit_length()
    masks = [(high & (1 << b)) != 0 for b in range(bits)]

    def find(tab, bit, start):
        if bit < 0:
            return jnp.take_along_axis(tab[first + start], low, axis=1)
        lower = find(tab, bit - 1, start)
        if start + (1 << bit) >= count:
            return lower
        return jnp.where(masks[bit], find(tab, bit - 1, start + (1 << bit)), lower)

    return [find(tab, bits - 1, 0) for tab in tabs]


def find_in_pool(tabs, own, tiles, index):
    low, high = index & (LANES - 1), index >> 7
    here = lookup(tabs, 0, own, low, high)
    there = lookup(tabs, own, tiles - own, low, high - own)
    return [jnp.where(high < own, a, b) for a, b in zip(here, there)]


def pair_index(near, pair, base):
    return jnp.where(
        upper_half(),
        row(near[2 * pair + 1 : 2 * pair + 2, pl.ds(base, LANES)]),
        row(near[2 * pair : 2 * pair + 1, pl.ds(base, LANES)]),
    )


def fill_exact(tab, block):
    for k in range(block.shape[1] // LANES):
        tab[k] = twice(block[:, k * LANES : (k + 1) * LANES])


def gather_ghosts(tab, comps, own, gs, out_first, out_last):
    width = out_first.shape[2]
    up = upper_half()
    for g in range(width // LANES):
        index = jnp.where(
            up,
            row(gs[:, width + g * LANES : width + (g + 1) * LANES]),
            row(gs[:, g * LANES : (g + 1) * LANES]),
        )
        found = lookup([tab.at[c] for c in range(comps)], 0, own, index & (LANES - 1), index >> 7)
        for c in range(comps):
            out_first[c, :, g * LANES : (g + 1) * LANES] = found[c][:4]
            out_last[c, :, g * LANES : (g + 1) * LANES] = found[c][4:]


def pack_params(tab, first, par):
    for k in range(par.shape[2] // LANES):
        cut = slice(k * LANES, (k + 1) * LANES)
        q = (par[0, :, cut] * Q_STEPS + 32768.5).astype(i32) - 32768
        e = (par[1, :, cut] * E_STEPS + 0.5).astype(i32)
        tab[first + k] = twice((q << 16) | e)


def largest(blocks):
    top = None
    for block in blocks:
        for c in range(3):
            here = jnp.max(jnp.abs(block[c]), axis=0, keepdims=True)
            here = jnp.max(here, axis=1, keepdims=True)
            top = here if top is None else jnp.maximum(top, here)
    return jnp.maximum(top, 1e-30)


def pack_positions(tabs, first, pos, top):
    factor = POS / top
    for k in range(pos.shape[2] // LANES):
        cut = slice(k * LANES, (k + 1) * LANES)
        x = (pos[0, :, cut] * factor + (1048576.5)).astype(i32) - 1048576
        y = (pos[1, :, cut] * factor + (1048576.5)).astype(i32) - 1048576
        z = (pos[2, :, cut] * factor * 2.0 + (2097152.5)).astype(i32)
        tabs[0][first + k] = twice((x << 11) | (z >> 11))
        tabs[1][first + k] = twice((y << 11) | (z & LOW))


def unpack_positions(words, unit):
    x = (words[0] >> 11).astype(f32) * unit
    y = (words[1] >> 11).astype(f32) * unit
    z = (((words[0] & LOW) << 11) | (words[1] & LOW)).astype(f32)
    return x, y, (z - 2097152.0) * (0.5 * unit)


def forces(pos, par, base, found, charges, depths):
    lanes = pl.ds(base, LANES)
    force = [[None] * 4 for _ in range(3)]
    for pair in range(len(charges)):
        there = found(pair)
        charge, depth = charges[pair], depths[pair]
        for i in range(4):
            offset = [row(pos[c, i : i + 1, lanes]) - there[c] for c in range(3)]
            square = offset[0] * offset[0] + offset[1] * offset[1] + offset[2] * offset[2]
            root = lax.rsqrt(square + softening)
            w = root * root
            qq = row(par[0, i : i + 1, lanes]) * charge
            ee = row(par[1, i : i + 1, lanes]) * depth
            weight = w * (qq * root + ee * (w * w - w))
            for c in range(3):
                term = weight * offset[c]
                force[c][i] = term if pair == 0 else force[c][i] + term
    return [
        jnp.concatenate([jnp.sum(force[c][i], axis=0, keepdims=True) for i in range(4)], 0)
        for c in range(3)
    ]


def kernel(
    partner, scale_order, coupling, phase, charges, lj, fill, near, gs, out,
    from_low, from_high, par, par_first, par_last, par_low, par_high,
    pos_first, pos_last, pos_low, pos_high, pos, pos_next, vel,
    exact, packed_par, packed_pos, gathered, part, send_sem, recv_sem,
):
    total, width = phase.shape[2], gs.shape[1] // 2
    own, ghost = total // LANES, width // LANES
    tiles = own + 2 * ghost
    pairs = near.shape[0] // 2
    level, levels = lax.axis_index("rep"), lax.axis_size("rep")
    place, places = lax.axis_index("space"), lax.axis_size("space")
    has_low, has_high = level > 0, level < levels - 1
    above, below = lax.rem(place + 1, places), lax.rem(place + places - 1, places)

    barrier = pltpu.get_barrier_semaphore()

    def greet(device):
        pl.semaphore_signal(barrier, inc=1, device_id=device, device_id_type=MESH)

    greet({"space": above})
    greet({"space": below})

    @pl.when(has_low)
    def _():
        greet({"rep": level - 1})

    @pl.when(has_high)
    def _():
        greet({"rep": level + 1})

    pl.semaphore_wait(barrier, 2 + jnp.where(has_low, 1, 0) + jnp.where(has_high, 1, 0))

    def remote(src, dst, number, device):
        return pltpu.make_async_remote_copy(
            src_ref=src, dst_ref=dst, send_sem=send_sem.at[number], recv_sem=recv_sem.at[number],
            device_id=device, device_id_type=MESH,
        )

    halves = (pl.ds(0, 3), pl.ds(3, 3))
    rising = [remote(phase.at[h], from_low.at[h], n, {"rep": level + 1}) for n, h in enumerate(halves)]
    falling = [remote(phase.at[h], from_high.at[h], 2 + n, {"rep": level - 1}) for n, h in enumerate(halves)]

    for n in range(2):

        @pl.when(has_high)
        def _():
            rising[n].start()

        @pl.when(has_low)
        def _():
            falling[n].start()

    def swap_arrived(n):
        @pl.when(has_low)
        def _():
            rising[n].wait_recv()

        @pl.when(has_high)
        def _():
            falling[n].wait_recv()

    def ring(first, last, low, high, number):
        return [remote(last, low, number, {"space": above}), remote(first, high, number + 1, {"space": below})]

    slot = lax.broadcasted_iota(i32, (4, total), 0)
    present = (slot < fill[...]).astype(f32)
    par[0] = charges[...] * present
    par[1] = lj[...] * present
    for c in range(2):
        fill_exact(exact.at[c], par[c])
    gather_ghosts(exact, 2, own, gs, par_first, par_last)
    par_ring = ring(par_first, par_last, par_low, par_high, 4)
    for copy in par_ring:
        copy.start()
    pack_params(packed_par, 0, par)
    early, ahead = own // 4, own * 5 // 8

    def each_group(start, stop, body):
        def step(group, carry):
            body(group, pl.multiple_of(group * LANES, LANES))
            return carry

        lax.fori_loop(start, stop, step, 0, unroll=2)

    def look_ahead(tabs):
        def body(group, base):
            for pair in range(pairs):
                index = pair_index(near, pair, base)
                words = lookup(tabs, 0, own, index & (LANES - 1), index >> 7)
                for n, word in enumerate(words):
                    part[group, pair, n] = word

        return body

    def find_rest(tabs, group, pair, index):
        words = lookup(tabs, own, tiles - own, index & (LANES - 1), (index >> 7) - own)
        return [jnp.where(index < total, part[group, pair, n], word) for n, word in enumerate(words)]

    each_group(0, early, look_ahead([packed_par]))

    moved = partner[level] - level

    def swapped(c, lanes):
        return jnp.where(
            moved == 0, phase[c, :, lanes],
            jnp.where(moved < 0, from_low[c, :, lanes], from_high[c, :, lanes]),
        )

    swap_arrived(0)
    for c in range(3):
        block = swapped(c, pl.ds(0, total))
        pos[c] = block
        fill_exact(exact.at[c], block)
    gather_ghosts(exact, 3, own, gs, pos_first.at[0], pos_last.at[0])
    pos_rings = [
        ring(pos_first.at[n], pos_last.at[n], pos_low.at[n], pos_high.at[n], 6 + 2 * n) for n in range(2)
    ]
    for copy in pos_rings[0]:
        copy.start()
    tabs = [packed_pos.at[0], packed_pos.at[1]]
    top_own = largest([pos])
    pack_positions(tabs, 0, pos, top_own)
    unit_own = top_own * (1.0 / POS)

    for copy in par_ring:
        copy.wait_recv()
    pack_params(packed_par, own, par_low)
    pack_params(packed_par, own + ghost, par_high)
    strength = coupling[scale_order[level]] * (1.0 / Q_STEPS)

    def keep_params(group, pair, word):
        gathered[group, pair, 0] = (word >> 16).astype(f32) * strength
        gathered[group, pair, 1] = (word & 65535).astype(f32) * (1.0 / E_STEPS)

    def finish_params(group, base):
        for pair in range(pairs):
            keep_params(group, pair, find_rest([packed_par], group, pair, pair_index(near, pair, base))[0])

    def gather_params(group, base):
        for pair in range(pairs):
            keep_params(group, pair, find_in_pool([packed_par], own, tiles, pair_index(near, pair, base))[0])

    each_group(0, early, finish_params)
    each_group(early, own, gather_params)

    def ghosts_arrived(n):
        for copy in pos_rings[n]:
            copy.wait_recv()
        low, high = pos_low.at[n], pos_high.at[n]
        top = largest([low, high])
        pack_positions(tabs, own, low, top)
        pack_positions(tabs, own + ghost, high, top)
        return top * (1.0 / POS)

    def params_of(group):
        return (
            [gathered[group, pair, 0] for pair in range(pairs)],
            [gathered[group, pair, 1] for pair in range(pairs)],
        )

    swap_arrived(1)
    unit_ghost = ghosts_arrived(0)

    def first_step(group, base):
        lanes = pl.ds(base, LANES)

        def found(pair):
            index = pair_index(near, pair, base)
            words = find_in_pool(tabs, own, tiles, index)
            return unpack_positions(words, jnp.where(index < total, unit_own, unit_ghost))

        force = forces(pos, par, base, found, *params_of(group))
        for c in range(3):
            v = swapped(3 + c, lanes) + time_step * force[c]
            vel[c, :, lanes] = v
            pos_next[c, :, lanes] = pos[c, :, lanes] + time_step * v

    each_group(0, own, first_step)

    for c in range(3):
        fill_exact(exact.at[c], pos_next[c])
    gather_ghosts(exact, 3, own, gs, pos_first.at[1], pos_last.at[1])
    for copy in pos_rings[1]:
        copy.start()
    top_own = largest([pos_next])
    pack_positions(tabs, 0, pos_next, top_own)
    unit_own_next = top_own * (1.0 / POS)

    each_group(0, ahead, look_ahead(tabs))
    unit_ghost_next = ghosts_arrived(1)

    def second_step(looked_up):
        def body(group, base):
            lanes = pl.ds(base, LANES)

            def found(pair):
                index = pair_index(near, pair, base)
                if looked_up:
                    words = find_rest(tabs, group, pair, index)
                else:
                    words = find_in_pool(tabs, own, tiles, index)
                return unpack_positions(words, jnp.where(index < total, unit_own_next, unit_ghost_next))

            force = forces(pos_next, par, base, found, *params_of(group))
            for c in range(3):
                v = vel[c, :, lanes] + time_step * force[c]
                out[3 + c, :, lanes] = v
                out[c, :, lanes] = pos_next[c, :, lanes] + time_step * v

        return body

    each_group(0, ahead, second_step(True))
    each_group(ahead, own, second_step(False))

    for copy in par_ring + pos_rings[0] + pos_rings[1]:
        copy.wait_send()
    for n in range(2):

        @pl.when(has_high)
        def _():
            rising[n].wait_send()

        @pl.when(has_low)
        def _():
            falling[n].wait_send()


def on_device(
    phase_space, charges, lj_depth, cluster_fill, neighbours, ghost_send, partner, scale_order, coupling
):
    phase = phase_space[0]
    rows, slots, total = phase.shape
    width = ghost_send.shape[1] // 2
    own = total // LANES
    tiles = own + 2 * (width // LANES)
    pairs = neighbours.shape[1] // 2
    out = pl.pallas_call(
        kernel,
        out_shape=jax.ShapeDtypeStruct(phase.shape, f32),
        in_specs=[SMEM] * 3 + [VMEM] * 6,
        out_specs=VMEM,
        scratch_shapes=[
            pltpu.VMEM((rows, slots, total), f32),
            pltpu.VMEM((rows, slots, total), f32),
            pltpu.VMEM((2, slots, total), f32),
        ]
        + [pltpu.VMEM((2, slots, width), f32)] * 4
        + [pltpu.VMEM((2, 3, slots, width), f32)] * 4
        + [pltpu.VMEM((3, slots, total), f32)] * 3
        + [
            pltpu.VMEM((3, own, 8, LANES), f32),
            pltpu.VMEM((tiles, 8, LANES), i32),
            pltpu.VMEM((2, tiles, 8, LANES), i32),
            pltpu.VMEM((own, pairs, 2, 8, LANES), f32),
            pltpu.VMEM((own, pairs, 2, 8, LANES), i32),
            pltpu.SemaphoreType.DMA((10,)),
            pltpu.SemaphoreType.DMA((10,)),
        ],
        compiler_params=pltpu.CompilerParams(collective_id=0, has_side_effects=True),
    )(partner, scale_order, coupling, phase, charges[0], lj_depth[0], cluster_fill, neighbours[0], ghost_send)
    return out[None]


def solution(mesh):
    return jax.shard_map(
        on_device,
        mesh=mesh,
        in_specs=(
            P("rep", None, None, "space"),
            P("rep", None, "space"),
            P("rep", None, "space"),
            P("rep", "space"),
            P("rep", None, "space"),
            P("rep", "space"),
            P(),
            P(),
            P(),
        ),
        out_specs=P("rep", None, None, "space"),
        check_vma=False,
    )
```
